32 devices in a mesh: outer: 4 (over x, core), inner: 8 (over z, y).
Axes of the slice: x: 2, y: 2, z: 4, core: 2. Of those that a mesh axis runs over, the one named last changes fastest.
Arguments:
- signal: bfloat16 [4096, 4096], P(('outer', 'inner')), may hold values from -6 to 6
- gating: bfloat16 [4096, 4096], P(('outer', 'inner')), may hold values from -6 to 6
- decay_rate: float32 [4096, 16], P('inner'), may hold values from 0.00012207031 to 0.05
- residues: float32 [4096, 16], P('inner'), may hold values from -1.5 to 1.5
- skip_gain: float32 [4096], replicated, may hold values from -3 to 3
Outputs:
- layer_out: bfloat16 [4096, 4096], P(('outer', 'inner'))
The draws below stay inside these ranges and needn't reach their ends.
All inputs are finite; a program needn't handle non-finite values.
Results may differ from the reference program's by a relative error of at most 0.001.
Values may be sent and summed in bfloat16 or wider, within the bound.
A program may use at most 128 MiB of HBM per device.

```python
import math
import jax
import jax.numpy as jnp
from jax import lax

D = 4096
MODES = 16
TOKENS = 4096


def levels(stream_key, dims, cuts, low, largest):
    def one(axis_at, parts):
        steps = jax.random.uniform(jax.random.fold_in(jax.random.fold_in(stream_key, 6), axis_at), (parts,), jnp.float32, low / len(cuts), largest / len(cuts))
        return jnp.repeat(jnp.exp(steps), dims[axis_at] // parts).reshape((-1,) + (1,) * (len(dims) - axis_at - 1))

    loudness = one(*cuts[0])
    for cut in cuts[1:]:
        loudness = loudness * one(*cut)
    return loudness


def gaussian(stream_key, extent, scale, most, split=(), kind=jnp.bfloat16):
    array = scale * jax.random.normal(stream_key, extent, jnp.float32)
    if split:
        array = array * levels(stream_key, extent, split, -0.22, 0.18)
    return jnp.clip(array, -most, most).astype(kind)


def setup_inputs(seed: int = 0) -> dict:
    streams_of = jax.random.split(jax.random.key(seed), 6)
    return {
        "signal": gaussian(streams_of[0], (TOKENS, D), 1.0, 6.0, ((0, 32),)),
        "gating": gaussian(streams_of[1], (TOKENS, D), 1.0, 6.0, ((0, 32),)),
        "decay_rate": jnp.clip(jnp.exp(math.log(0.05) - 6.015181 * jax.random.uniform(streams_of[2], (D, MODES), jnp.float32) ** levels(streams_of[2], (D, MODES), ((0, 8),), -0.2, 0.2)), 0.00012207031, 0.05),
        "residues": gaussian(streams_of[3], (D, MODES), 0.25, 1.5, ((0, 8),), jnp.float32),
        "skip_gain": gaussian(streams_of[4], (D,), 0.5, 3.0, (), jnp.float32),
    }


def filter_spectrum(frequency, padded, seq_length, decay_rate, residues):
    angles = frequency.astype(jnp.float32) * (2.0 * math.pi / padded)
    sine_half = jnp.sin(0.5 * angles)
    bending = 2.0 * sine_half * sine_half
    sine_full = jnp.sin(angles)
    parity = (1 - 2 * (frequency % 2)).astype(jnp.float32)
    zeros_out = jnp.zeros_like(angles + decay_rate[:, 0])

    def add_mode(mode_index, totals):
        real_sum, imag_sum = totals
        mode_rate = lax.dynamic_index_in_dim(decay_rate, mode_index, 1, keepdims=False)
        weights = lax.dynamic_index_in_dim(residues, mode_index, 1, keepdims=False)
        decays = jnp.exp(-mode_rate)
        scaled = weights * jnp.sqrt(-jnp.expm1(-2.0 * mode_rate))
        numerator = scaled * (1.0 - jnp.exp(-seq_length * mode_rate) * parity)
        den_real = -jnp.expm1(-mode_rate) + decays * bending
        den_imag = decays * sine_full
        quotient = numerator / (den_real * den_real + den_imag * den_imag)
        return (real_sum + quotient * den_real, imag_sum - quotient * den_imag)
    return lax.fori_loop(0, decay_rate.shape[1], add_mode, (zeros_out, zeros_out))

def reference(signal, gating, decay_rate, residues, skip_gain):
    padded = 2 * TOKENS
    block_width = math.gcd(D, 256)
    block_count = D // block_width
    frequency = jnp.arange(padded, dtype=jnp.int32)[:, None]
    signal_f = signal.astype(jnp.float32)
    blocks_in = signal_f.reshape(TOKENS, block_count, block_width).transpose(1, 0, 2)
    rate_blocks = decay_rate.reshape(block_count, block_width, MODES)
    residue_blocks = residues.reshape(block_count, block_width, MODES)

    def convolve(operands):
        block_signal, block_rate, block_residue = operands
        spectrum = jnp.fft.fft(block_signal, n=padded, axis=0)
        filter_re, filter_im = filter_spectrum(frequency, padded, TOKENS, block_rate, block_residue)
        product = spectrum * lax.complex(filter_re, filter_im)
        return jnp.real(jnp.fft.ifft(product, axis=0)[:TOKENS])
    convolved = lax.map(convolve, (blocks_in, rate_blocks, residue_blocks))
    convolved = convolved.transpose(1, 0, 2).reshape(TOKENS, D)
    return (gating.astype(jnp.float32) * (convolved + skip_gain[None, :] * signal_f)).astype(jnp.bfloat16)
```

```python
import functools

import jax
import jax.numpy as jnp
from jax import lax
from jax.experimental import pallas as pl
from jax.experimental.pallas import tpu as pltpu
from jax.sharding import PartitionSpec as P

MESH = pl.DeviceIdType.MESH
LANES = 128
SUB = 8


def wrap(value, size):
    return lax.rem(value + size, size)


def tree_sum(terms):
    terms = list(terms)
    while len(terms) > 1:
        paired = [terms[i] + terms[i + 1] for i in range(0, len(terms) - 1, 2)]
        if len(terms) % 2:
            paired.append(terms[-1])
        terms = paired
    return terms[0]


def kernel(
    groups, inner, modes,
    par_ref, signal_ref, gating_ref, skip_ref, out_ref,
    par_buf, x_buf, y_buf, state_in, weight_in, state_out, state_got, carry_out,
    carry_got, total_buf, tap_buf,
    par_send, par_recv, state_send, state_recv, carry_send, carry_recv,
    total_send, total_recv,
):
    me = lax.axis_index("inner")
    block = lax.axis_index("outer")
    rows, channels = signal_ref.shape
    width = par_ref.shape[1]
    tiles = width // LANES
    steps = rows // SUB
    full = (SUB, LANES)
    seg = lax.broadcasted_iota(jnp.int32, full, 0)
    seg_f = seg.astype(jnp.float32)

    barrier = pltpu.get_barrier_semaphore()

    @pl.loop(1, inner)
    def _(r):
        pl.semaphore_signal(
            barrier, inc=1, device_id={"inner": wrap(me + r, inner)}, device_id_type=MESH
        )

    @pl.loop(1, groups)
    def _(r):
        pl.semaphore_signal(
            barrier, inc=1, device_id={"outer": wrap(block + r, groups)}, device_id_type=MESH
        )

    pl.semaphore_wait(barrier, inner + groups - 2)

    def par_copy(r):
        return pltpu.make_async_remote_copy(
            src_ref=par_ref, dst_ref=par_buf.at[r],
            send_sem=par_send.at[r], recv_sem=par_recv.at[r],
            device_id={"inner": wrap(me + r, inner)}, device_id_type=MESH,
        )

    def state_copy(r):
        return pltpu.make_async_remote_copy(
            src_ref=state_out.at[r], dst_ref=state_got.at[r],
            send_sem=state_send.at[r], recv_sem=state_recv.at[r],
            device_id={"inner": wrap(me - r, inner)}, device_id_type=MESH,
        )

    def carry_copy(r):
        return pltpu.make_async_remote_copy(
            src_ref=carry_out.at[r], dst_ref=carry_got.at[r],
            send_sem=carry_send.at[r], recv_sem=carry_recv.at[r],
            device_id={"inner": wrap(me + r, inner)}, device_id_type=MESH,
        )

    def total_copy(r):
        return pltpu.make_async_remote_copy(
            src_ref=total_buf.at[0], dst_ref=total_buf.at[r],
            send_sem=total_send.at[r], recv_sem=total_recv.at[r],
            device_id={"outer": wrap(block + r, groups)}, device_id_type=MESH,
        )

    @pl.loop(1, inner)
    def _(r):
        par_copy(r).start()

    par_buf[0] = par_ref[...]

    def place(r, tile):
        start = wrap(me - r, inner) * width + tile * LANES
        return (
            pl.ds(pl.multiple_of(start, LANES), LANES),
            pl.ds(pl.multiple_of(tile * LANES, LANES), LANES),
        )

    def rate_row(r, m, local):
        return jnp.broadcast_to(par_buf[r, m : m + 1, local], full)

    def weight_row(r, m, local):
        return jnp.broadcast_to(par_buf[r, modes + m : modes + m + 1, local], full)

    def end_states(r, tile):
        cols, local = place(r, tile)
        slot = r * tiles + tile
        x_buf[slot] = signal_ref[:, cols].astype(jnp.float32)
        rates = par_buf[r, 0:modes, local]
        for power, scale in enumerate((1.0, steps, 2.0 * steps, 4.0 * steps)):
            tap_buf[power * modes : (power + 1) * modes, :] = jnp.exp(rates * (-scale))

        def row(power, m):
            at = power * modes + m
            return jnp.broadcast_to(tap_buf[at : at + 1, :], full)

        decays = [row(0, m) for m in range(modes)]
        first = x_buf[slot, pl.ds(0, SUB, stride=steps), :]
        states = [first] * modes
        for j in range(1, steps):
            value = x_buf[slot, pl.ds(j, SUB, stride=steps), :]
            states = [decays[m] * states[m] + value for m in range(modes)]
        for m in range(modes):
            ends = states[m]
            for power, hop in ((1, 1), (2, 2), (3, 4)):
                moved = jnp.where(seg >= hop, pltpu.roll(ends, hop, 0), 0.0)
                ends = ends + row(power, m) * moved
            state_in[slot, m] = ends
            state_out[r, m : m + 1, local] = ends[SUB - 1 : SUB, :]

    def within(r, tile):
        cols, local = place(r, tile)
        slot = r * tiles + tile
        taps = [jnp.zeros(full, jnp.float32) for _ in range(steps // SUB)]
        for m in range(modes):
            rate = rate_row(r, m, local)
            weight = weight_row(r, m, local)
            for part in range(steps // SUB):
                taps[part] = taps[part] + weight * jnp.exp(-rate * (seg_f + float(part * SUB)))
            ends = jnp.where(seg >= 1, pltpu.roll(state_in[slot, m], 1, 0), 0.0)
            state_in[slot, m] = ends * (weight * jnp.exp(-rate))
            weight_in[slot, m] = weight * jnp.exp(-rate * (seg_f * float(steps) + 1.0))
        for part in range(steps // SUB):
            tap_buf[part * SUB : (part + 1) * SUB, :] = taps[part]
        values = [x_buf[slot, pl.ds(j, SUB, stride=steps), :] for j in range(steps)]
        filters = [jnp.broadcast_to(tap_buf[j : j + 1, :], full) for j in range(steps)]
        for j in range(steps):
            y_buf[slot, pl.ds(j, SUB, stride=steps), :] = tree_sum(
                [filters[k] * values[j - k] for k in range(j + 1)]
            )

    def finish(r, tile):
        cols, local = place(r, tile)
        slot = r * tiles + tile
        terms = []
        decays = []
        for m in range(modes):
            carry = jnp.broadcast_to(carry_got[r, m : m + 1, local], full)
            terms.append(state_in[slot, m] + weight_in[slot, m] * carry)
        tap_buf[0:modes, :] = jnp.exp(-par_buf[r, 0:modes, local])
        decays = [jnp.broadcast_to(tap_buf[m : m + 1, :], full) for m in range(modes)]
        for j in range(steps):
            at = pl.ds(j, SUB, stride=steps)
            y_buf[slot, at, :] = y_buf[slot, at, :] + tree_sum(terms)
            if j + 1 < steps:
                terms = [terms[m] * decays[m] for m in range(modes)]
        skip = jnp.broadcast_to(skip_ref[:, cols], (2 * SUB, LANES))
        for part in range(rows // (2 * SUB)):
            at = slice(part * 2 * SUB, (part + 1) * 2 * SUB)
            gate = gating_ref[at, cols].astype(jnp.float32)
            out_ref[at, cols] = (
                gate * (y_buf[slot, at, :] + skip * x_buf[slot, at, :])
            ).astype(jnp.bfloat16)

    def sweep(low, high, body):
        @pl.loop(low * tiles, high * tiles)
        def _(i):
            body(i // tiles, i % tiles)

    @pl.loop(0, inner)
    def _(r):
        @pl.when(r > 0)
        def _():
            par_copy(r).wait_recv()

        @pl.loop(0, tiles)
        def _(tile):
            end_states(r, tile)

        @pl.when(r > 0)
        def _():
            state_copy(r).start()

    cut_a = inner // 2
    cut_b = (3 * inner) // 4
    sweep(0, cut_a, within)

    @pl.loop(1, inner)
    def _(r):
        state_copy(r).wait_recv()

    state_got[0] = state_out[0]
    rates = par_buf[0, 0:modes, :]
    decay_block = jnp.exp(rates * (-float(rows)))

    def advance(b, run):
        at = wrap(b - me, inner)
        carry_out[at] = run
        return decay_block * run + state_got[at]

    total = lax.fori_loop(0, inner, advance, jnp.zeros((modes, width), jnp.float32))
    total_buf[0] = total

    @pl.loop(1, groups)
    def _(r):
        total_copy(r).start()

    sweep(cut_a, cut_b, within)

    @pl.loop(1, groups)
    def _(r):
        total_copy(r).wait_recv()

    decay_group = jnp.exp(rates * (-float(rows * inner)))

    def join(b, run):
        got = total_buf[wrap(block - b, groups)]
        return jnp.where(b < block, decay_group * run + got, run)

    before = lax.fori_loop(0, groups, join, jnp.zeros((modes, width), jnp.float32))

    @pl.loop(0, inner)
    def _(r):
        b = wrap(me + r, inner)
        reach = (b * (-rows)).astype(jnp.float32)
        carry_out[r] = carry_out[r] + jnp.exp(rates * reach) * before

        @pl.when(r > 0)
        def _():
            carry_copy(r).start()

    carry_got[0] = carry_out[0]
    sweep(cut_b, inner, within)

    @pl.loop(0, inner)
    def _(r):
        @pl.when(r > 0)
        def _():
            carry_copy(r).wait_recv()

        @pl.loop(0, tiles)
        def _(tile):
            finish(r, tile)

    @pl.loop(1, inner)
    def _(r):
        par_copy(r).wait_send()
        state_copy(r).wait_send()
        carry_copy(r).wait_send()

    @pl.loop(1, groups)
    def _(r):
        total_copy(r).wait_send()


def per_device(signal, gating, decay_rate, residues, skip_gain):
    groups = lax.axis_size("outer")
    inner = lax.axis_size("inner")
    rows, channels = signal.shape
    width, modes = decay_rate.shape
    tiles = width // LANES
    weights = residues * jnp.sqrt(-jnp.expm1(-2.0 * decay_rate))
    params = jnp.concatenate([decay_rate.T, weights.T], axis=0)
    f32 = jnp.float32
    dma = pltpu.SemaphoreType.DMA
    part = (inner, modes, width)
    return pl.pallas_call(
        functools.partial(kernel, groups, inner, modes),
        out_shape=jax.ShapeDtypeStruct((rows, channels), jnp.bfloat16),
        in_specs=[pl.BlockSpec(memory_space=pltpu.VMEM)] * 4,
        out_specs=pl.BlockSpec(memory_space=pltpu.VMEM),
        scratch_shapes=[
            pltpu.VMEM((inner, 2 * modes, width), f32),
            pltpu.VMEM((inner * tiles, rows, LANES), f32),
            pltpu.VMEM((inner * tiles, rows, LANES), f32),
            pltpu.VMEM((inner * tiles, modes, SUB, LANES), f32),
            pltpu.VMEM((inner * tiles, modes, SUB, LANES), f32),
            pltpu.VMEM(part, f32),
            pltpu.VMEM(part, f32),
            pltpu.VMEM(part, f32),
            pltpu.VMEM(part, f32),
            pltpu.VMEM((groups, modes, width), f32),
            pltpu.VMEM((4 * modes, LANES), f32),
            dma((inner,)), dma((inner,)), dma((inner,)), dma((inner,)),
            dma((inner,)), dma((inner,)), dma((groups,)), dma((groups,)),
        ],
        compiler_params=pltpu.CompilerParams(
            collective_id=0, has_side_effects=True, vmem_limit_bytes=40 * 1024 * 1024
        ),
        name="modal_scan",
    )(params, signal, gating, skip_gain[None, :])


def solution(mesh):
    return jax.shard_map(
        per_device,
        mesh=mesh,
        in_specs=(
            P(("outer", "inner"), None),
            P(("outer", "inner"), None),
            P("inner", None),
            P("inner", None),
            P(),
        ),
        out_specs=P(("outer", "inner"), None),
        check_vma=False,
    )
```

```python
import functools

import jax
import jax.numpy as jnp
from jax import lax
from jax.experimental import pallas as pl
from jax.experimental.pallas import tpu as pltpu
from jax.sharding import PartitionSpec as P

MESH = pl.DeviceIdType.MESH
LANES = 128
SUB = 8


def wrap(value, size):
    return lax.rem(value + size, size)


def tree_sum(terms):
    terms = list(terms)
    while len(terms) > 1:
        paired = [terms[i] + terms[i + 1] for i in range(0, len(terms) - 1, 2)]
        if len(terms) % 2:
            paired.append(terms[-1])
        terms = paired
    return terms[0]


def one_minus_exp(z):
    series = jnp.ones_like(z)
    for n in range(12, 1, -1):
        series = 1.0 - series * z * (1.0 / n)
    return jnp.where(z < 0.5, z * series, 1.0 - jnp.exp(-z))


def kernel(
    groups, inner, modes,
    rate_hbm, residue_hbm, signal_hbm, gating_hbm, skip_hbm, out_ref,
    rate_ref, residue_ref, signal_ref, gating_ref, skip_ref,
    par_buf, x_buf, y_buf, state_in, weight_in, state_out, state_got, carry_out,
    carry_got, total_buf, tap_buf,
    load_sem, par_send, par_recv, core_send, core_recv, state_send, state_recv,
    carry_send, carry_recv, total_send, total_recv,
):
    me = lax.axis_index("inner")
    block = lax.axis_index("outer")
    half = lax.rem(block, 2)
    twin = block + 1 - 2 * half
    rows, channels = signal_ref.shape
    width = rate_ref.shape[1]
    tiles = width // LANES
    steps = rows // SUB
    full = (SUB, LANES)
    seg = lax.broadcasted_iota(jnp.int32, full, 0)
    seg_f = seg.astype(jnp.float32)

    barrier = pltpu.get_barrier_semaphore()

    @pl.loop(1, inner)
    def _(r):
        pl.semaphore_signal(
            barrier, inc=1, device_id={"inner": wrap(me + r, inner)}, device_id_type=MESH
        )

    @pl.loop(1, groups)
    def _(r):
        pl.semaphore_signal(
            barrier, inc=1, device_id={"outer": wrap(block + r, groups)}, device_id_type=MESH
        )

    loads = [
        pltpu.make_async_copy(source, target, load_sem.at[n])
        for n, (source, target) in enumerate((
            (rate_hbm, rate_ref), (residue_hbm, residue_ref), (signal_hbm, signal_ref),
            (gating_hbm, gating_ref), (skip_hbm, skip_ref),
        ))
    ]
    for load in loads:
        load.start()

    def remote(source, target, send, recv, device):
        return pltpu.make_async_remote_copy(
            src_ref=source, dst_ref=target, send_sem=send, recv_sem=recv,
            device_id=device, device_id_type=MESH,
        )

    def par_copy(r):
        return remote(
            par_buf.at[0, half], par_buf.at[r, half],
            par_send.at[r], par_recv.at[r], {"inner": wrap(me + r, inner)},
        )

    def par_core(r):
        return remote(
            par_buf.at[r, half], par_buf.at[r, half],
            core_send.at[r], core_recv.at[r], {"outer": twin},
        )

    def state_copy(r):
        return remote(
            state_out.at[r], state_got.at[r],
            state_send.at[r], state_recv.at[r], {"inner": wrap(me - r, inner)},
        )

    def carry_copy(r):
        return remote(
            carry_out.at[r], carry_got.at[r],
            carry_send.at[r], carry_recv.at[r], {"inner": wrap(me + r, inner)},
        )

    def total_copy(r):
        return remote(
            total_buf.at[0], total_buf.at[r],
            total_send.at[r], total_recv.at[r], {"outer": wrap(block + r, groups)},
        )

    loads[0].wait()
    loads[1].wait()
    par_buf[0, 0] = rate_ref[...]
    par_buf[0, 1] = residue_ref[...] * jnp.sqrt(one_minus_exp(2.0 * rate_ref[...]))
    pl.semaphore_wait(barrier, inner + groups - 2)

    @pl.loop(1, inner)
    def _(r):
        par_copy(r).start()

    def place(slot, tile):
        start = wrap(me - slot, inner) * width + tile * LANES
        return (
            pl.ds(pl.multiple_of(start, LANES), LANES),
            pl.ds(pl.multiple_of(tile * LANES, LANES), LANES),
        )

    def rate_row(r, m, local):
        return jnp.broadcast_to(par_buf[r, 0, m : m + 1, local], full)

    def weight_row(r, m, local):
        return jnp.broadcast_to(par_buf[r, 1, m : m + 1, local], full)

    def end_states(r, tile):
        cols, local = place(r, tile)
        slot = r * tiles + tile
        x_buf[slot] = signal_ref[:, cols].astype(jnp.float32)
        rates = par_buf[r, 0, :, local]
        for power, scale in enumerate((1.0, steps, 2.0 * steps, 4.0 * steps)):
            tap_buf[power * modes : (power + 1) * modes, :] = jnp.exp(rates * (-scale))

        def row(power, m):
            at = power * modes + m
            return jnp.broadcast_to(tap_buf[at : at + 1, :], full)

        decays = [row(0, m) for m in range(modes)]
        first = x_buf[slot, pl.ds(0, SUB, stride=steps), :]
        states = [first] * modes
        for j in range(1, steps):
            value = x_buf[slot, pl.ds(j, SUB, stride=steps), :]
            states = [decays[m] * states[m] + value for m in range(modes)]
        for m in range(modes):
            ends = states[m]
            for power, hop in ((1, 1), (2, 2), (3, 4)):
                moved = jnp.where(seg >= hop, pltpu.roll(ends, hop, 0), 0.0)
                ends = ends + row(power, m) * moved
            state_in[slot, m] = ends
            state_out[r, m : m + 1, local] = ends[SUB - 1 : SUB, :]

    def within(r, tile):
        cols, local = place(r, tile)
        slot = r * tiles + tile
        taps = [jnp.zeros(full, jnp.float32) for _ in range(steps // SUB)]
        for m in range(modes):
            rate = rate_row(r, m, local)
            weight = weight_row(r, m, local)
            for part in range(steps // SUB):
                taps[part] = taps[part] + weight * jnp.exp(-rate * (seg_f + float(part * SUB)))
            ends = jnp.where(seg >= 1, pltpu.roll(state_in[slot, m], 1, 0), 0.0)
            state_in[slot, m] = ends * (weight * jnp.exp(-rate))
            weight_in[slot, m] = weight * jnp.exp(-rate * (seg_f * float(steps) + 1.0))
        for part in range(steps // SUB):
            tap_buf[part * SUB : (part + 1) * SUB, :] = taps[part]
        values = [x_buf[slot, pl.ds(j, SUB, stride=steps), :] for j in range(steps)]
        filters = [jnp.broadcast_to(tap_buf[j : j + 1, :], full) for j in range(steps)]
        for j in range(steps):
            y_buf[slot, pl.ds(j, SUB, stride=steps), :] = tree_sum(
                [filters[k] * values[j - k] for k in range(j + 1)]
            )

    def finish(r, tile):
        cols, local = place(r, tile)
        slot = r * tiles + tile
        terms = []
        decays = []
        for m in range(modes):
            carry = jnp.broadcast_to(carry_got[r, m : m + 1, local], full)
            terms.append(state_in[slot, m] + weight_in[slot, m] * carry)
        tap_buf[0:modes, :] = jnp.exp(-par_buf[r, 0, :, local])
        decays = [jnp.broadcast_to(tap_buf[m : m + 1, :], full) for m in range(modes)]
        for j in range(steps):
            at = pl.ds(j, SUB, stride=steps)
            y_buf[slot, at, :] = y_buf[slot, at, :] + tree_sum(terms)
            if j + 1 < steps:
                terms = [terms[m] * decays[m] for m in range(modes)]
        skip = jnp.broadcast_to(skip_ref[:, cols], (2 * SUB, LANES))
        for part in range(rows // (2 * SUB)):
            at = slice(part * 2 * SUB, (part + 1) * 2 * SUB)
            gate = gating_ref[at, cols].astype(jnp.float32)
            out_ref[at, cols] = (
                gate * (y_buf[slot, at, :] + skip * x_buf[slot, at, :])
            ).astype(jnp.bfloat16)

    def sweep(low, high, body):
        @pl.loop(low * tiles, high * tiles)
        def _(i):
            body(i // tiles, i % tiles)

    def end_slot(slot):
        @pl.loop(0, tiles)
        def _(tile):
            end_states(slot, tile)

    loads[2].wait()
    end_slot(0)
    par_copy(1).wait_recv()
    par_core(1).start()

    @pl.loop(1, inner)
    def _(r):
        @pl.when(r + 1 < inner)
        def _():
            par_copy(r + 1).wait_recv()
            par_core(r + 1).start()

        par_core(r).wait_recv()
        end_slot(r)
        state_copy(r).start()

    cut_a = inner // 2
    cut_b = (3 * inner) // 4
    sweep(0, cut_a, within)

    @pl.loop(1, inner)
    def _(r):
        state_copy(r).wait_recv()

    state_got[0] = state_out[0]
    rates = par_buf[0, 0]
    decay_block = jnp.exp(rates * (-float(rows)))

    def advance(b, run):
        at = wrap(b - me, inner)
        carry_out[at] = run
        return decay_block * run + state_got[at]

    total = lax.fori_loop(0, inner, advance, jnp.zeros((modes, width), jnp.float32))
    total_buf[0] = total

    @pl.loop(1, groups)
    def _(r):
        total_copy(r).start()

    sweep(cut_a, cut_b, within)

    @pl.loop(1, groups)
    def _(r):
        total_copy(r).wait_recv()

    decay_group = jnp.exp(rates * (-float(rows * inner)))

    def join(b, run):
        got = total_buf[wrap(block - b, groups)]
        return jnp.where(b < block, decay_group * run + got, run)

    before = lax.fori_loop(0, groups, join, jnp.zeros((modes, width), jnp.float32))

    @pl.loop(0, inner)
    def _(r):
        b = wrap(me + r, inner)
        reach = (b * (-rows)).astype(jnp.float32)
        carry_out[r] = carry_out[r] + jnp.exp(rates * reach) * before

        @pl.when(r > 0)
        def _():
            carry_copy(r).start()

    carry_got[0] = carry_out[0]
    sweep(cut_b, inner, within)
    loads[3].wait()
    loads[4].wait()

    @pl.loop(0, inner)
    def _(r):
        @pl.when(r > 0)
        def _():
            carry_copy(r).wait_recv()

        @pl.loop(0, tiles)
        def _(tile):
            finish(r, tile)

    @pl.loop(1, inner)
    def _(r):
        par_copy(r).wait_send()
        par_core(r).wait_send()
        state_copy(r).wait_send()
        carry_copy(r).wait_send()

    @pl.loop(1, groups)
    def _(r):
        total_copy(r).wait_send()


def per_device(signal, gating, decay_rate, residues, skip_gain):
    groups = lax.axis_size("outer")
    inner = lax.axis_size("inner")
    rows, channels = signal.shape
    width, modes = decay_rate.shape
    tiles = width // LANES
    f32 = jnp.float32
    dma = pltpu.SemaphoreType.DMA

    def states(count):
        return pltpu.VMEM((count, modes, width), f32)

    return pl.pallas_call(
        functools.partial(kernel, groups, inner, modes),
        out_shape=jax.ShapeDtypeStruct((rows, channels), jnp.bfloat16),
        in_specs=[pl.BlockSpec(memory_space=pltpu.HBM)] * 5,
        out_specs=pl.BlockSpec(memory_space=pltpu.VMEM),
        scratch_shapes=[
            pltpu.VMEM((modes, width), f32),
            pltpu.VMEM((modes, width), f32),
            pltpu.VMEM((rows, channels), jnp.bfloat16),
            pltpu.VMEM((rows, channels), jnp.bfloat16),
            pltpu.VMEM((1, channels), f32),
            pltpu.VMEM((inner, 2, modes, width), f32),
            pltpu.VMEM((inner * tiles, rows, LANES), f32),
            pltpu.VMEM((inner * tiles, rows, LANES), f32),
            pltpu.VMEM((inner * tiles, modes, SUB, LANES), f32),
            pltpu.VMEM((inner * tiles, modes, SUB, LANES), f32),
            states(inner), states(inner), states(inner), states(inner), states(groups),
            pltpu.VMEM((4 * modes, LANES), f32),
            dma((5,)), dma((inner,)), dma((inner,)), dma((inner,)), dma((inner,)), dma((inner,)),
            dma((inner,)), dma((inner,)), dma((inner,)), dma((groups,)), dma((groups,)),
        ],
        compiler_params=pltpu.CompilerParams(
            collective_id=0, has_side_effects=True, vmem_limit_bytes=63 * 1024 * 1024
        ),
        name="modal_scan",
    )(decay_rate.T, residues.T, signal, gating, skip_gain[None, :])


def solution(mesh):
    return jax.shard_map(
        per_device,
        mesh=mesh,
        in_specs=(
            P(("outer", "inner"), None),
            P(("outer", "inner"), None),
            P("inner", None),
            P("inner", None),
            P(),
        ),
        out_specs=P(("outer", "inner"), None),
        check_vma=False,
    )
```

```python
import functools

import jax
import jax.numpy as jnp
from jax import lax
from jax.experimental import pallas as pl
from jax.experimental.pallas import tpu as pltpu
from jax.sharding import PartitionSpec as P

MESH = pl.DeviceIdType.MESH
LANES = 128
SUB = 8
CHUNKS = 1


def wrap(value, size):
    return lax.rem(value + size, size)


def tree_sum(terms):
    terms = list(terms)
    while len(terms) > 1:
        paired = [terms[i] + terms[i + 1] for i in range(0, len(terms) - 1, 2)]
        if len(terms) % 2:
            paired.append(terms[-1])
        terms = paired
    return terms[0]


def one_minus_exp(z):
    series = jnp.ones_like(z)
    for n in range(12, 1, -1):
        series = 1.0 - series * z * (1.0 / n)
    return jnp.where(z < 0.5, z * series, 1.0 - jnp.exp(-z))


def kernel(
    groups, inner, modes,
    rate_hbm, residue_hbm, signal_hbm, gating_hbm, skip_hbm, out_hbm,
    rate_ref, residue_ref, signal_ref, gating_ref, skip_ref,
    out_buf, par_buf, x_buf, y_buf, state_in, weight_in, state_out, state_got, carry_out,
    carry_got, total_buf, tap_buf,
    load_sem, out_sem, par_send, par_recv, core_send, core_recv, state_send, state_recv,
    carry_send, carry_recv, total_send, total_recv,
):
    me = lax.axis_index("inner")
    block = lax.axis_index("outer")
    half = lax.rem(block, 2)
    twin = block + 1 - 2 * half
    rows, channels = signal_ref.shape
    width = rate_ref.shape[1]
    tiles = width // LANES
    steps = rows // SUB
    part = modes // CHUNKS
    full = (SUB, LANES)
    seg = lax.broadcasted_iota(jnp.int32, full, 0)
    seg_f = seg.astype(jnp.float32)

    barrier = pltpu.get_barrier_semaphore()

    @pl.loop(1, inner)
    def _(r):
        pl.semaphore_signal(
            barrier, inc=1, device_id={"inner": wrap(me + r, inner)}, device_id_type=MESH
        )

    @pl.loop(1, groups)
    def _(r):
        pl.semaphore_signal(
            barrier, inc=1, device_id={"outer": wrap(block + r, groups)}, device_id_type=MESH
        )

    loads = [
        pltpu.make_async_copy(source, target, load_sem.at[n])
        for n, (source, target) in enumerate((
            (rate_hbm, rate_ref), (residue_hbm, residue_ref), (signal_hbm, signal_ref),
            (gating_hbm, gating_ref), (skip_hbm, skip_ref),
        ))
    ]
    for load in loads:
        load.start()

    def remote(source, target, send, recv, device):
        return pltpu.make_async_remote_copy(
            src_ref=source, dst_ref=target, send_sem=send, recv_sem=recv,
            device_id=device, device_id_type=MESH,
        )

    def par_copy(c, r):
        return remote(
            par_buf.at[c, 0, half], par_buf.at[c, r, half],
            par_send.at[c, r], par_recv.at[c, r], {"inner": wrap(me + r, inner)},
        )

    def par_core(c, r):
        return remote(
            par_buf.at[c, r, half], par_buf.at[c, r, half],
            core_send.at[c, r], core_recv.at[c, r], {"outer": twin},
        )

    def state_copy(c, r):
        return remote(
            state_out.at[c, r], state_got.at[c, r],
            state_send.at[c, r], state_recv.at[c, r], {"inner": wrap(me - r, inner)},
        )

    def carry_copy(c, r):
        return remote(
            carry_out.at[c, r], carry_got.at[c, r],
            carry_send.at[c, r], carry_recv.at[c, r], {"inner": wrap(me + r, inner)},
        )

    def total_copy(c, r):
        return remote(
            total_buf.at[c, 0], total_buf.at[c, r],
            total_send.at[c, r], total_recv.at[c, r], {"outer": wrap(block + r, groups)},
        )

    def out_copy(slot):
        start = wrap(me - slot, inner) * width
        cols = pl.ds(pl.multiple_of(start, LANES), width)
        return pltpu.make_async_copy(
            out_buf.at[:, cols], out_hbm.at[:, cols], out_sem.at[slot]
        )

    loads[0].wait()
    loads[1].wait()
    for c in range(CHUNKS):
        at = slice(c * part, (c + 1) * part)
        par_buf[c, 0, 0] = rate_ref[at]
        par_buf[c, 0, 1] = residue_ref[at] * jnp.sqrt(one_minus_exp(2.0 * rate_ref[at]))
    pl.semaphore_wait(barrier, inner + groups - 2)

    for c in range(CHUNKS):
        @pl.loop(1, inner)
        def _(r):
            par_copy(c, r).start()

    def place(slot, tile):
        start = wrap(me - slot, inner) * width + tile * LANES
        return (
            pl.ds(pl.multiple_of(start, LANES), LANES),
            pl.ds(pl.multiple_of(tile * LANES, LANES), LANES),
        )

    def rate_row(r, m, local):
        at = m % part
        return jnp.broadcast_to(par_buf[m // part, r, 0, at : at + 1, local], full)

    def weight_row(r, m, local):
        at = m % part
        return jnp.broadcast_to(par_buf[m // part, r, 1, at : at + 1, local], full)

    def end_states(c, r, tile):
        cols, local = place(r, tile)
        slot = r * tiles + tile
        rates = par_buf[c, r, 0, :, local]
        for power, scale in enumerate((1.0, steps, 2.0 * steps, 4.0 * steps)):
            tap_buf[power * part : (power + 1) * part, :] = jnp.exp(rates * (-scale))

        def row(power, m):
            at = power * part + m
            return jnp.broadcast_to(tap_buf[at : at + 1, :], full)

        decays = [row(0, m) for m in range(part)]
        first = x_buf[slot, pl.ds(0, SUB, stride=steps), :]
        states = [first] * part
        for j in range(1, steps):
            value = x_buf[slot, pl.ds(j, SUB, stride=steps), :]
            states = [decays[m] * states[m] + value for m in range(part)]
        for m in range(part):
            ends = states[m]
            for power, hop in ((1, 1), (2, 2), (3, 4)):
                moved = jnp.where(seg >= hop, pltpu.roll(ends, hop, 0), 0.0)
                ends = ends + row(power, m) * moved
            state_in[slot, c * part + m] = ends
            state_out[c, r, m : m + 1, local] = ends[SUB - 1 : SUB, :]

    def within(r, tile):
        cols, local = place(r, tile)
        slot = r * tiles + tile
        taps = [jnp.zeros(full, jnp.float32) for _ in range(steps // SUB)]
        for m in range(modes):
            rate = rate_row(r, m, local)
            weight = weight_row(r, m, local)
            for n in range(steps // SUB):
                taps[n] = taps[n] + weight * jnp.exp(-rate * (seg_f + float(n * SUB)))
            ends = jnp.where(seg >= 1, pltpu.roll(state_in[slot, m], 1, 0), 0.0)
            state_in[slot, m] = ends * (weight * jnp.exp(-rate))
            weight_in[slot, m] = weight * jnp.exp(-rate * (seg_f * float(steps) + 1.0))
        for n in range(steps // SUB):
            tap_buf[n * SUB : (n + 1) * SUB, :] = taps[n]
        values = [x_buf[slot, pl.ds(j, SUB, stride=steps), :] for j in range(steps)]
        filters = [jnp.broadcast_to(tap_buf[j : j + 1, :], full) for j in range(steps)]
        for j in range(steps):
            y_buf[slot, pl.ds(j, SUB, stride=steps), :] = tree_sum(
                [filters[k] * values[j - k] for k in range(j + 1)]
            )

    def finish(r, tile):
        cols, local = place(r, tile)
        slot = r * tiles + tile
        terms = []
        decays = []
        for m in range(modes):
            at = m % part
            carry = jnp.broadcast_to(carry_got[m // part, r, at : at + 1, local], full)
            terms.append(state_in[slot, m] + weight_in[slot, m] * carry)
        for c in range(CHUNKS):
            tap_buf[c * part : (c + 1) * part, :] = jnp.exp(-par_buf[c, r, 0, :, local])
        decays = [jnp.broadcast_to(tap_buf[m : m + 1, :], full) for m in range(modes)]
        for j in range(steps):
            at = pl.ds(j, SUB, stride=steps)
            y_buf[slot, at, :] = y_buf[slot, at, :] + tree_sum(terms)
            if j + 1 < steps:
                terms = [terms[m] * decays[m] for m in range(modes)]
        skip = jnp.broadcast_to(skip_ref[:, cols], (2 * SUB, LANES))
        for n in range(rows // (2 * SUB)):
            at = slice(n * 2 * SUB, (n + 1) * 2 * SUB)
            gate = gating_ref[at, cols].astype(jnp.float32)
            out_buf[at, cols] = (
                gate * (y_buf[slot, at, :] + skip * x_buf[slot, at, :])
            ).astype(jnp.bfloat16)

    def sweep(low, high, body):
        @pl.loop(low * tiles, high * tiles)
        def _(i):
            body(i // tiles, i % tiles)

    def end_slot(c, r):
        @pl.loop(0, tiles)
        def _(tile):
            end_states(c, r, tile)

    def widen(r):
        @pl.loop(0, tiles)
        def _(tile):
            cols, local = place(r, tile)
            x_buf[r * tiles + tile] = signal_ref[:, cols].astype(jnp.float32)

    loads[2].wait()
    widen(0)
    for c in range(CHUNKS):
        end_slot(c, 0)

    def relay(c, r):
        par_copy(c, r).wait_recv()
        par_core(c, r).start()

    relay(0, 1)
    for c in range(CHUNKS):
        @pl.loop(1, inner)
        def _(r):
            @pl.when(r + 1 < inner)
            def _():
                relay(c, r + 1)

            if c + 1 < CHUNKS:
                @pl.when(r + 1 == inner)
                def _():
                    relay(c + 1, 1)

            if c == 0:
                widen(r)
            par_core(c, r).wait_recv()
            end_slot(c, r)
            state_copy(c, r).start()

    nothing = jnp.zeros((part, width), jnp.float32)

    def gather_total(c):
        @pl.loop(1, inner)
        def _(r):
            state_copy(c, r).wait_recv()

        state_got[c, 0] = state_out[c, 0]
        decay_block = jnp.exp(par_buf[c, 0, 0] * (-float(rows)))

        def advance(b, run):
            at = wrap(b - me, inner)
            carry_out[c, at] = run
            return decay_block * run + state_got[c, at]

        total_buf[c, 0] = lax.fori_loop(0, inner, advance, nothing)

        @pl.loop(1, groups)
        def _(r):
            total_copy(c, r).start()

    def give_carries(c):
        @pl.loop(1, groups)
        def _(r):
            total_copy(c, r).wait_recv()

        rates = par_buf[c, 0, 0]
        decay_group = jnp.exp(rates * (-float(rows * inner)))

        def join(b, run):
            got = total_buf[c, wrap(block - b, groups)]
            return jnp.where(b < block, decay_group * run + got, run)

        before = lax.fori_loop(0, groups, join, nothing)

        @pl.loop(0, inner)
        def _(r):
            b = wrap(me + r, inner)
            reach = (b * (-rows)).astype(jnp.float32)
            carry_out[c, r] = carry_out[c, r] + jnp.exp(rates * reach) * before

            @pl.when(r > 0)
            def _():
                carry_copy(c, r).start()

        carry_got[c, 0] = carry_out[c, 0]

    cuts = [0, inner // 4, inner // 2, (3 * inner) // 4, inner]
    gather_total(0)
    sweep(cuts[0], cuts[1], within)
    for c in range(1, CHUNKS):
        gather_total(c)
    sweep(cuts[1], cuts[2], within)
    give_carries(0)
    for c in range(1, CHUNKS):
        give_carries(c)
    sweep(cuts[2], cuts[4], within)
    loads[3].wait()
    loads[4].wait()

    @pl.loop(0, inner)
    def _(r):
        @pl.when(r > 0)
        def _():
            for c in range(CHUNKS):
                carry_copy(c, r).wait_recv()

        @pl.loop(0, tiles)
        def _(tile):
            finish(r, tile)

        out_copy(r).start()

    for c in range(CHUNKS):
        @pl.loop(1, inner)
        def _(r):
            par_copy(c, r).wait_send()
            par_core(c, r).wait_send()
            state_copy(c, r).wait_send()
            carry_copy(c, r).wait_send()

        @pl.loop(1, groups)
        def _(r):
            total_copy(c, r).wait_send()

    @pl.loop(0, inner)
    def _(r):
        out_copy(r).wait()


def per_device(signal, gating, decay_rate, residues, skip_gain):
    groups = lax.axis_size("outer")
    inner = lax.axis_size("inner")
    rows, channels = signal.shape
    width, modes = decay_rate.shape
    tiles = width // LANES
    f32 = jnp.float32
    dma = pltpu.SemaphoreType.DMA

    part = modes // CHUNKS

    def states(count):
        return pltpu.VMEM((CHUNKS, count, part, width), f32)

    return pl.pallas_call(
        functools.partial(kernel, groups, inner, modes),
        out_shape=jax.ShapeDtypeStruct((rows, channels), jnp.bfloat16),
        in_specs=[pl.BlockSpec(memory_space=pltpu.HBM)] * 5,
        out_specs=pl.BlockSpec(memory_space=pltpu.HBM),
        scratch_shapes=[
            pltpu.VMEM((modes, width), f32),
            pltpu.VMEM((modes, width), f32),
            pltpu.VMEM((rows, channels), jnp.bfloat16),
            pltpu.VMEM((rows, channels), jnp.bfloat16),
            pltpu.VMEM((1, channels), f32),
            pltpu.VMEM((rows, channels), jnp.bfloat16),
            pltpu.VMEM((CHUNKS, inner, 2, part, width), f32),
            pltpu.VMEM((inner * tiles, rows, LANES), f32),
            pltpu.VMEM((inner * tiles, rows, LANES), f32),
            pltpu.VMEM((inner * tiles, modes, SUB, LANES), f32),
            pltpu.VMEM((inner * tiles, modes, SUB, LANES), f32),
            states(inner), states(inner), states(inner), states(inner), states(groups),
            pltpu.VMEM((4 * modes, LANES), f32),
            dma((5,)), dma((inner,)),
            *[dma((CHUNKS, inner)) for _ in range(8)],
            dma((CHUNKS, groups)), dma((CHUNKS, groups)),
        ],
        compiler_params=pltpu.CompilerParams(
            collective_id=0, has_side_effects=True, vmem_limit_bytes=63 * 1024 * 1024
        ),
        name="modal_scan",
    )(decay_rate.T, residues.T, signal, gating, skip_gain[None, :])


def solution(mesh):
    return jax.shard_map(
        per_device,
        mesh=mesh,
        in_specs=(
            P(("outer", "inner"), None),
            P(("outer", "inner"), None),
            P("inner", None),
            P("inner", None),
            P(),
        ),
        out_specs=P(("outer", "inner"), None),
        check_vma=False,
    )
```

```python
import functools

import jax
import jax.numpy as jnp
from jax import lax
from jax.experimental import pallas as pl
from jax.experimental.pallas import tpu as pltpu
from jax.sharding import PartitionSpec as P

MESH = pl.DeviceIdType.MESH
LANES = 128
SUB = 8
CHUNKS = 1


def wrap(value, size):
    return lax.rem(value + size, size)


def tree_sum(terms):
    terms = list(terms)
    while len(terms) > 1:
        paired = [terms[i] + terms[i + 1] for i in range(0, len(terms) - 1, 2)]
        if len(terms) % 2:
            paired.append(terms[-1])
        terms = paired
    return terms[0]


def one_minus_exp(z):
    series = jnp.ones_like(z)
    for n in range(12, 1, -1):
        series = 1.0 - series * z * (1.0 / n)
    return jnp.where(z < 0.5, z * series, 1.0 - jnp.exp(-z))


def kernel(
    groups, inner, modes,
    rate_hbm, residue_hbm, signal_hbm, gating_hbm, skip_hbm, out_hbm,
    rate_ref, residue_ref, signal_ref, gating_ref, skip_ref,
    out_buf, par_buf, x_buf, y_buf, state_in, weight_in, state_out, state_got, carry_out,
    carry_got, total_buf, tap_buf,
    load_sem, out_sem, par_send, par_recv, core_send, core_recv, state_send, state_recv,
    carry_send, carry_recv, total_send, total_recv,
):
    me = lax.axis_index("inner")
    block = lax.axis_index("outer")
    half = lax.rem(block, 2)
    twin = block + 1 - 2 * half
    rows, channels = signal_ref.shape
    width = rate_ref.shape[1]
    tiles = width // LANES
    steps = rows // SUB
    part = modes // CHUNKS
    full = (SUB, LANES)
    seg = lax.broadcasted_iota(jnp.int32, full, 0)
    seg_f = seg.astype(jnp.float32)

    barrier = pltpu.get_barrier_semaphore()

    @pl.loop(1, inner)
    def _(r):
        pl.semaphore_signal(
            barrier, inc=1, device_id={"inner": wrap(me + r, inner)}, device_id_type=MESH
        )

    @pl.loop(1, groups)
    def _(r):
        pl.semaphore_signal(
            barrier, inc=1, device_id={"outer": wrap(block + r, groups)}, device_id_type=MESH
        )

    loads = [
        pltpu.make_async_copy(source, target, load_sem.at[n])
        for n, (source, target) in enumerate((
            (rate_hbm, rate_ref), (residue_hbm, residue_ref), (signal_hbm, signal_ref),
            (gating_hbm, gating_ref), (skip_hbm, skip_ref),
        ))
    ]
    for load in loads:
        load.start()

    def remote(source, target, send, recv, device):
        return pltpu.make_async_remote_copy(
            src_ref=source, dst_ref=target, send_sem=send, recv_sem=recv,
            device_id=device, device_id_type=MESH,
        )

    def par_copy(c, r):
        return remote(
            par_buf.at[c, 0, half], par_buf.at[c, r, half],
            par_send.at[c, r], par_recv.at[c, r], {"inner": wrap(me + r, inner)},
        )

    def par_core(c, r):
        return remote(
            par_buf.at[c, r, half], par_buf.at[c, r, half],
            core_send.at[c, r], core_recv.at[c, r], {"outer": twin},
        )

    def state_copy(c, r):
        return remote(
            state_out.at[c, r], state_got.at[c, r],
            state_send.at[c, r], state_recv.at[c, r], {"inner": wrap(me - r, inner)},
        )

    def carry_copy(c, r):
        return remote(
            carry_out.at[c, r], carry_got.at[c, r],
            carry_send.at[c, r], carry_recv.at[c, r], {"inner": wrap(me + r, inner)},
        )

    def total_copy(c, r):
        return remote(
            total_buf.at[c, 0], total_buf.at[c, r],
            total_send.at[c, r], total_recv.at[c, r], {"outer": wrap(block + r, groups)},
        )

    def out_copy(slot):
        start = wrap(me - slot, inner) * width
        cols = pl.ds(pl.multiple_of(start, LANES), width)
        return pltpu.make_async_copy(
            out_buf.at[:, cols], out_hbm.at[:, cols], out_sem.at[slot]
        )

    loads[0].wait()
    loads[1].wait()
    for c in range(CHUNKS):
        at = slice(c * part, (c + 1) * part)
        par_buf[c, 0, 0] = rate_ref[at]
        par_buf[c, 0, 1] = residue_ref[at] * jnp.sqrt(one_minus_exp(2.0 * rate_ref[at]))
    pl.semaphore_wait(barrier, inner + groups - 2)

    def order(k):
        return (k + 1) // 2 + (1 - k % 2) * (inner - k)

    for c in range(CHUNKS):
        @pl.loop(1, inner)
        def _(r):
            par_copy(c, order(r)).start()

    def place(slot, tile):
        start = wrap(me - slot, inner) * width + tile * LANES
        return (
            pl.ds(pl.multiple_of(start, LANES), LANES),
            pl.ds(pl.multiple_of(tile * LANES, LANES), LANES),
        )

    def rate_row(r, m, local):
        at = m % part
        return jnp.broadcast_to(par_buf[m // part, r, 0, at : at + 1, local], full)

    def weight_row(r, m, local):
        at = m % part
        return jnp.broadcast_to(par_buf[m // part, r, 1, at : at + 1, local], full)

    def end_states(c, r, tile):
        cols, local = place(r, tile)
        slot = r * tiles + tile
        rates = par_buf[c, r, 0, :, local]
        for power, scale in enumerate((1.0, steps, 2.0 * steps, 4.0 * steps)):
            tap_buf[power * part : (power + 1) * part, :] = jnp.exp(rates * (-scale))

        def row(power, m):
            at = power * part + m
            return jnp.broadcast_to(tap_buf[at : at + 1, :], full)

        decays = [row(0, m) for m in range(part)]
        first = x_buf[slot, pl.ds(0, SUB, stride=steps), :]
        states = [first] * part
        for j in range(1, steps):
            value = x_buf[slot, pl.ds(j, SUB, stride=steps), :]
            states = [decays[m] * states[m] + value for m in range(part)]
        for m in range(part):
            ends = states[m]
            for power, hop in ((1, 1), (2, 2), (3, 4)):
                moved = jnp.where(seg >= hop, pltpu.roll(ends, hop, 0), 0.0)
                ends = ends + row(power, m) * moved
            state_in[slot, c * part + m] = ends
            state_out[c, r, m : m + 1, local] = ends[SUB - 1 : SUB, :]

    def within(r, tile):
        cols, local = place(r, tile)
        slot = r * tiles + tile
        taps = [jnp.zeros(full, jnp.float32) for _ in range(steps // SUB)]
        for m in range(modes):
            rate = rate_row(r, m, local)
            weight = weight_row(r, m, local)
            for n in range(steps // SUB):
                taps[n] = taps[n] + weight * jnp.exp(-rate * (seg_f + float(n * SUB)))
            ends = jnp.where(seg >= 1, pltpu.roll(state_in[slot, m], 1, 0), 0.0)
            state_in[slot, m] = ends * (weight * jnp.exp(-rate))
            weight_in[slot, m] = weight * jnp.exp(-rate * (seg_f * float(steps) + 1.0))
        for n in range(steps // SUB):
            tap_buf[n * SUB : (n + 1) * SUB, :] = taps[n]
        values = [x_buf[slot, pl.ds(j, SUB, stride=steps), :] for j in range(steps)]
        filters = [jnp.broadcast_to(tap_buf[j : j + 1, :], full) for j in range(steps)]
        for j in range(steps):
            y_buf[slot, pl.ds(j, SUB, stride=steps), :] = tree_sum(
                [filters[k] * values[j - k] for k in range(j + 1)]
            )

    def finish(r, tile):
        cols, local = place(r, tile)
        slot = r * tiles + tile
        terms = []
        decays = []
        for m in range(modes):
            at = m % part
            carry = jnp.broadcast_to(carry_got[m // part, r, at : at + 1, local], full)
            terms.append(state_in[slot, m] + weight_in[slot, m] * carry)
        for c in range(CHUNKS):
            tap_buf[c * part : (c + 1) * part, :] = jnp.exp(-par_buf[c, r, 0, :, local])
        decays = [jnp.broadcast_to(tap_buf[m : m + 1, :], full) for m in range(modes)]
        for j in range(steps):
            at = pl.ds(j, SUB, stride=steps)
            y_buf[slot, at, :] = y_buf[slot, at, :] + tree_sum(terms)
            if j + 1 < steps:
                terms = [terms[m] * decays[m] for m in range(modes)]
        skip = jnp.broadcast_to(skip_ref[:, cols], (2 * SUB, LANES))
        for n in range(rows // (2 * SUB)):
            at = slice(n * 2 * SUB, (n + 1) * 2 * SUB)
            gate = gating_ref[at, cols].astype(jnp.float32)
            out_buf[at, cols] = (
                gate * (y_buf[slot, at, :] + skip * x_buf[slot, at, :])
            ).astype(jnp.bfloat16)

    def sweep(low, high, body):
        @pl.loop(low * tiles, high * tiles)
        def _(i):
            body(i // tiles, i % tiles)

    def end_slot(c, r):
        @pl.loop(0, tiles)
        def _(tile):
            end_states(c, r, tile)

    def widen(r):
        @pl.loop(0, tiles)
        def _(tile):
            cols, local = place(r, tile)
            x_buf[r * tiles + tile] = signal_ref[:, cols].astype(jnp.float32)

    loads[2].wait()
    widen(0)
    for c in range(CHUNKS):
        end_slot(c, 0)

    def relay(c, r):
        par_copy(c, r).wait_recv()
        par_core(c, r).start()

    relay(0, 1)
    for c in range(CHUNKS):
        @pl.loop(1, inner)
        def _(r):
            @pl.when(r + 1 < inner)
            def _():
                relay(c, order(r + 1))

            if c + 1 < CHUNKS:
                @pl.when(r + 1 == inner)
                def _():
                    relay(c + 1, 1)

            at = order(r)
            if c == 0:
                widen(at)
            par_core(c, at).wait_recv()
            end_slot(c, at)
            state_copy(c, at).start()

    nothing = jnp.zeros((part, width), jnp.float32)

    def gather_total(c):
        @pl.loop(1, inner)
        def _(r):
            state_copy(c, r).wait_recv()

        state_got[c, 0] = state_out[c, 0]
        decay_block = jnp.exp(par_buf[c, 0, 0] * (-float(rows)))

        def advance(b, run):
            at = wrap(b - me, inner)
            carry_out[c, at] = run
            return decay_block * run + state_got[c, at]

        total_buf[c, 0] = lax.fori_loop(0, inner, advance, nothing)

        @pl.loop(1, groups)
        def _(r):
            total_copy(c, r).start()

    def give_carries(c):
        @pl.loop(1, groups)
        def _(r):
            total_copy(c, r).wait_recv()

        rates = par_buf[c, 0, 0]
        decay_group = jnp.exp(rates * (-float(rows * inner)))

        def join(b, run):
            got = total_buf[c, wrap(block - b, groups)]
            return jnp.where(b < block, decay_group * run + got, run)

        before = lax.fori_loop(0, groups, join, nothing)

        @pl.loop(0, inner)
        def _(r):
            b = wrap(me + r, inner)
            reach = (b * (-rows)).astype(jnp.float32)
            carry_out[c, r] = carry_out[c, r] + jnp.exp(rates * reach) * before

            @pl.when(r > 0)
            def _():
                carry_copy(c, r).start()

        carry_got[c, 0] = carry_out[c, 0]

    cuts = [0, inner // 4, inner // 2, (3 * inner) // 4, inner]
    gather_total(0)
    sweep(cuts[0], cuts[1], within)
    for c in range(1, CHUNKS):
        gather_total(c)
    sweep(cuts[1], cuts[2], within)
    give_carries(0)
    for c in range(1, CHUNKS):
        give_carries(c)
    sweep(cuts[2], cuts[4], within)
    loads[3].wait()
    loads[4].wait()

    @pl.loop(0, inner)
    def _(r):
        @pl.when(r > 0)
        def _():
            for c in range(CHUNKS):
                carry_copy(c, r).wait_recv()

        @pl.loop(0, tiles)
        def _(tile):
            finish(r, tile)

        out_copy(r).start()

    for c in range(CHUNKS):
        @pl.loop(1, inner)
        def _(r):
            par_copy(c, r).wait_send()
            par_core(c, r).wait_send()
            state_copy(c, r).wait_send()
            carry_copy(c, r).wait_send()

        @pl.loop(1, groups)
        def _(r):
            total_copy(c, r).wait_send()

    @pl.loop(0, inner)
    def _(r):
        out_copy(r).wait()


def per_device(signal, gating, decay_rate, residues, skip_gain):
    groups = lax.axis_size("outer")
    inner = lax.axis_size("inner")
    rows, channels = signal.shape
    width, modes = decay_rate.shape
    tiles = width // LANES
    f32 = jnp.float32
    dma = pltpu.SemaphoreType.DMA

    part = modes // CHUNKS

    def states(count):
        return pltpu.VMEM((CHUNKS, count, part, width), f32)

    return pl.pallas_call(
        functools.partial(kernel, groups, inner, modes),
        out_shape=jax.ShapeDtypeStruct((rows, channels), jnp.bfloat16),
        in_specs=[pl.BlockSpec(memory_space=pltpu.HBM)] * 5,
        out_specs=pl.BlockSpec(memory_space=pltpu.HBM),
        scratch_shapes=[
            pltpu.VMEM((modes, width), f32),
            pltpu.VMEM((modes, width), f32),
            pltpu.VMEM((rows, channels), jnp.bfloat16),
            pltpu.VMEM((rows, channels), jnp.bfloat16),
            pltpu.VMEM((1, channels), f32),
            pltpu.VMEM((rows, channels), jnp.bfloat16),
            pltpu.VMEM((CHUNKS, inner, 2, part, width), f32),
            pltpu.VMEM((inner * tiles, rows, LANES), f32),
            pltpu.VMEM((inner * tiles, rows, LANES), f32),
            pltpu.VMEM((inner * tiles, modes, SUB, LANES), f32),
            pltpu.VMEM((inner * tiles, modes, SUB, LANES), f32),
            states(inner), states(inner), states(inner), states(inner), states(groups),
            pltpu.VMEM((4 * modes, LANES), f32),
            dma((5,)), dma((inner,)),
            *[dma((CHUNKS, inner)) for _ in range(8)],
            dma((CHUNKS, groups)), dma((CHUNKS, groups)),
        ],
        compiler_params=pltpu.CompilerParams(
            collective_id=0, has_side_effects=True, vmem_limit_bytes=63 * 1024 * 1024
        ),
        name="modal_scan",
    )(decay_rate.T, residues.T, signal, gating, skip_gain[None, :])


def solution(mesh):
    return jax.shard_map(
        per_device,
        mesh=mesh,
        in_specs=(
            P(("outer", "inner"), None),
            P(("outer", "inner"), None),
            P("inner", None),
            P("inner", None),
            P(),
        ),
        out_specs=P(("outer", "inner"), None),
        check_vma=False,
    )
```
